32 devices in a mesh: grp: 2 (over x), seq: 16 (over z, y, core).
Axes of the slice: x: 2, y: 2, z: 4, core: 2. Of those that a mesh axis runs over, the one named last changes fastest.
Arguments:
- hidden: bfloat16 [4, 5120, 1280], P('grp', 'seq'), parts along dimension 0, may hold values from -160 to 160
- mod_shift: float32 [5120], replicated, may hold values from -3 to 3
- mod_scale: float32 [5120], replicated, may hold values from -0.5 to 0.5
- head_weight: float32 [64, 5120], replicated, may hold values from -0.078125 to 0.078125
- head_bias: float32 [64], replicated, may hold values from -3 to 3
- conv_in_weight: bfloat16 [3, 3, 3, 16, 384], replicated, may hold values from -0.3125 to 0.3125
- conv_in_bias: float32 [384], replicated, may hold values from -3 to 3
- gain_in: float32 [384], replicated, may hold values from 0.1 to 1.9
- up_weight: bfloat16 [3, 3, 384, 192], replicated, may hold values from -0.109375 to 0.109375
- up_bias: float32 [192], replicated, may hold values from -3 to 3
- gain_up: float32 [192], replicated, may hold values from 0.1 to 1.9
- out_weight: bfloat16 [3, 3, 3, 192, 96], replicated, may hold values from -0.078125 to 0.078125
- out_bias: float32 [96], replicated, may hold values from -2 to 2
Outputs:
- decoded: bfloat16 [4, 64, 320, 96], P('grp', 'seq'), parts along dimension 0
The draws below stay inside these ranges and needn't reach their ends.
There are 2 independent parts, one for each index of `grp`. The reference program is written for one: setup_inputs(seed, part) draws one part's arguments, and reference() takes and returns one part's arrays. A program takes and returns all parts, laid end to end along the dimension named above; an argument that names none is the same for every part. Nothing has to cross between parts.
All inputs are finite; a program needn't handle non-finite values.
Results may differ from the reference program's by a relative error of at most 0.0056.
Values may be sent and summed in bfloat16 or wider, within the bound.
A program may use at most 64 MiB of HBM per device.

```python
import math
import jax
import jax.numpy as jnp
from jax import lax

D = 5120
LAT = 16
C1 = 384
C2 = 192
C3 = 96
FRAMES = 2
TOK_W = 80
PATCH = 64
TOK_ROWS = 16


def draw_hidden(key, part):
    key_base = jax.random.fold_in(key, 11)
    key_rows = jax.random.fold_in(key, 12)
    key_cols = jax.random.fold_in(key, 13)
    shape_all = (FRAMES, D, TOK_ROWS * TOK_W)
    row_scale = jnp.exp(jax.random.uniform(key_rows, (FRAMES, 1, TOK_ROWS * TOK_W), minval=0.0, maxval=math.log(10.0)))
    col_jitter = jnp.exp(jax.random.uniform(key_cols, (1, D, 1), minval=0.0, maxval=math.log(2.0)))
    position = (jnp.arange(D, dtype=jnp.float32) / D).reshape(1, D, 1)
    base_vals = jnp.clip(jax.random.normal(key_base, shape_all), -4.0, 4.0)
    col_scale = 10.0 ** position * col_jitter * 0.5
    result = base_vals * row_scale * col_scale * 0.3
    return jnp.clip(result, -160.0, 160.0).astype(jnp.bfloat16)


def bell_draw(own_key, extent, deviation, reach, kind=jnp.bfloat16):
    drawn = jax.random.normal(own_key, extent, jnp.float32) * deviation
    return jnp.minimum(jnp.maximum(drawn, -reach), reach).astype(kind)


def setup_inputs(seed: int = 0, part: int = 0) -> dict:
    key_list = jax.random.split(jax.random.key(seed), 14)
    own_keys = jax.random.split(jax.random.fold_in(key_list[13], part), 14)
    return {
        "hidden": draw_hidden(jax.random.fold_in(jax.random.fold_in(key_list[13], part), 71), part),
        "mod_shift": bell_draw(key_list[1], (D,), 0.5, 3.0, jnp.float32),
        "mod_scale": jnp.clip(jax.random.uniform(key_list[2], (D,), jnp.float32, -0.5, 0.5), -0.5, 0.5),
        "head_weight": bell_draw(key_list[3], (PATCH, D), D ** -0.5, 0.078125, jnp.float32),
        "head_bias": bell_draw(key_list[4], (PATCH,), 0.5, 3.0, jnp.float32),
        "conv_in_weight": bell_draw(key_list[5], (3, 3, 3, LAT, C1), (27 * LAT) ** -0.5, 0.3125),
        "conv_in_bias": bell_draw(key_list[6], (C1,), 0.5, 3.0, jnp.float32),
        "gain_in": jnp.clip(1.0 + 0.18 * jax.random.normal(key_list[7], (C1,), jnp.float32), 0.1, 1.9),
        "up_weight": bell_draw(key_list[8], (3, 3, C1, C2), (9 * C1) ** -0.5, 0.109375),
        "up_bias": bell_draw(key_list[9], (C2,), 0.5, 3.0, jnp.float32),
        "gain_up": jnp.clip(1.0 + 0.18 * jax.random.normal(key_list[10], (C2,), jnp.float32), 0.1, 1.9),
        "out_weight": bell_draw(key_list[11], (3, 3, 3, C2, C3), (27 * C2) ** -0.5, 0.078125),
        "out_bias": bell_draw(key_list[12], (C3,), 0.3, 2.0, jnp.float32),
    }


def rms_silu(values, gain_vec):
    squares = lax.optimization_barrier(jnp.mean(values * values, axis=-1, keepdims=True))
    normed = values * lax.rsqrt(squares + 1e-06) * gain_vec
    return normed * jax.nn.sigmoid(normed)

def conv_time(values, weight):
    padded = jnp.pad(values, ((2, 0), (1, 1), (1, 1), (0, 0))).astype(jnp.float32)
    result = lax.conv_general_dilated(padded[None], weight.astype(jnp.float32), (1, 1, 1), 'VALID', dimension_numbers=('NDHWC', 'DHWIO', 'NDHWC'), precision=lax.Precision.HIGHEST)
    return result[0]

def conv_plane(values, weight):
    padded = jnp.pad(values, ((0, 0), (1, 1), (1, 1), (0, 0))).astype(jnp.float32)
    return lax.conv_general_dilated(padded, weight.astype(jnp.float32), (1, 1), 'VALID', dimension_numbers=('NHWC', 'HWIO', 'NHWC'), precision=lax.Precision.HIGHEST)

def unpatch(projected):
    frames, tok_rows, tok_cols, patch_len = projected.shape
    lat_ch = patch_len // 4
    grid = projected.reshape(frames, tok_rows, tok_cols, 2, 2, lat_ch)
    return grid.transpose(0, 1, 3, 2, 4, 5).reshape(frames, 2 * tok_rows, 2 * tok_cols, lat_ch)

def reference(hidden, mod_shift, mod_scale, head_weight, head_bias, conv_in_weight, conv_in_bias, gain_in, up_weight, up_bias, gain_up, out_weight, out_bias):
    values = hidden.astype(jnp.float32)
    token_mean = lax.optimization_barrier(jnp.mean(values, axis=1, keepdims=True))
    centred = values - token_mean
    variance = lax.optimization_barrier(jnp.mean(centred * centred, axis=1, keepdims=True))
    modded = centred * lax.rsqrt(variance + 1e-06) * (1.0 + mod_scale)[:, None] + mod_shift[:, None]
    projected = jnp.einsum('fdt,kd->ftk', modded, head_weight, precision=lax.Precision.HIGHEST) + head_bias
    projected = projected.reshape(FRAMES, TOK_ROWS, TOK_W, PATCH)
    latent = unpatch(projected.astype(jnp.bfloat16))
    first_act = rms_silu(conv_time(latent, conv_in_weight) + conv_in_bias, gain_in).astype(jnp.bfloat16)
    upsampled = jnp.repeat(jnp.repeat(first_act, 2, axis=1), 2, axis=2)
    second_act = rms_silu(conv_plane(upsampled, up_weight) + up_bias, gain_up).astype(jnp.bfloat16)
    return (conv_time(second_act, out_weight) + out_bias).astype(jnp.bfloat16)
```

```python
import functools

import jax
import jax.numpy as jnp
from jax import lax
from jax.experimental import pallas as pl
from jax.experimental.pallas import tpu as pltpu
from jax.sharding import PartitionSpec as P

TOK_W = 80
HIGH = lax.Precision.HIGHEST
F32 = jnp.float32
BF16 = jnp.bfloat16


def rms_silu(values, gain_vec):
    squares = jnp.mean(values * values, axis=-1, keepdims=True)
    normed = values * lax.rsqrt(squares + 1e-06) * gain_vec
    return normed * jax.nn.sigmoid(normed)


def shift_cols(values, step):
    count = values.shape[0]
    col = lax.broadcasted_iota(jnp.int32, (count, 1), 0) % TOK_W
    if step > 0:
        return jnp.where(col == 0, 0.0, pltpu.roll(values, 1, 0))
    return jnp.where(col == TOK_W - 1, 0.0, pltpu.roll(values, count - 1, 0))


def conv_kernel(num_dev, lat_rows, chans, pos_ref, x_ref, w1_ref, b1_ref, g1_ref, w2_ref, b2_ref, g2_ref,
                w3_ref, b3_ref, out_ref, act1, act2, res):
    c1, c2, c3 = chans
    dev = pos_ref[0]
    rows1 = lat_rows + 2
    m1 = rows1 * TOK_W
    rows2 = lat_rows + 1
    m2 = rows2 * TOK_W
    rows3 = 2 * lat_rows
    m3 = rows3 * TOK_W

    def inside(count, first, step, total):
        row = lax.broadcasted_iota(jnp.int32, (count, 1), 0) // TOK_W * step + first
        return (row >= 0) & (row < total)

    keep1 = inside(m1, dev * lat_rows - 1, 1, num_dev * lat_rows)
    for frame in range(2):
        x_now = x_ref[frame].reshape(m1, x_ref.shape[-1])
        pre = jnp.dot(x_now, w1_ref[1], preferred_element_type=F32)
        if frame == 1:
            x_old = x_ref[0].reshape(m1, x_ref.shape[-1])
            pre = pre + jnp.dot(x_old, w1_ref[0], preferred_element_type=F32)
        for r in range(2):
            val = rms_silu(pre[:, r * c1 : (r + 1) * c1] + b1_ref[...], g1_ref[...])
            val = jnp.where(keep1, val, 0.0)
            edge = shift_cols(val, 1) if r == 1 else shift_cols(val, -1)
            spot = 0 if r == 1 else 3
            act1[frame, :, :, (r + 1) * c1 : (r + 2) * c1] = val.astype(BF16).reshape(rows1, TOK_W, c1)
            act1[frame, :, :, spot * c1 : (spot + 1) * c1] = edge.astype(BF16).reshape(rows1, TOK_W, c1)

    start = (0, 1, 1, 2)
    for p in range(2):
        first = 0 if p == 0 else -1
        keep2 = inside(m2, 2 * dev * lat_rows + first, 2, 2 * num_dev * lat_rows)
        for frame in range(2):
            for s in range(4):
                q = s % 2
                lanes = slice(start[s] * c1, (start[s] + 2) * c1)
                top = act1[frame, 0:rows2, :, lanes].reshape(m2, 2 * c1)
                low = act1[frame, 1 : rows2 + 1, :, lanes].reshape(m2, 2 * c1)
                pre = jnp.dot(top, w2_ref[p, 0, q], preferred_element_type=F32)
                pre = pre + jnp.dot(low, w2_ref[p, 1, q], preferred_element_type=F32)
                val = rms_silu(pre + b2_ref[...], g2_ref[...])
                val = jnp.where(keep2, val, 0.0)
                val = jnp.concatenate([val, jnp.zeros((m2, 256 - c2), F32)], axis=1)
                pieces = [(s + 1, val)]
                if s == 3:
                    pieces.append((0, shift_cols(val, 1)))
                if s == 0:
                    pieces.append((5, shift_cols(val, -1)))
                for spot, piece in pieces:
                    piece = piece.astype(BF16).reshape(rows2, TOK_W, 256)
                    for i in range(rows2):
                        act2[frame, 2 * i + 1 - p, :, spot * 256 : (spot + 1) * 256] = piece[i]

    for s in range(4):
        lanes = slice(s * 256, (s + 3) * 256)
        old = None
        new = None
        for b in range(3):
            before = act2[0, b : b + rows3, :, lanes].reshape(m3, 768)
            after = act2[1, b : b + rows3, :, lanes].reshape(m3, 768)
            one = jnp.dot(before, w3_ref[b], preferred_element_type=F32)
            two = jnp.dot(after, w3_ref[b, :, 0:128], preferred_element_type=F32)
            old = one if old is None else old + one
            new = two if new is None else new + two
        res[pl.ds(s, m3, stride=4), :] = old[:, 0:128] + b3_ref[...]
        res[pl.ds(4 * m3 + s, m3, stride=4), :] = old[:, 128:256] + new + b3_ref[...]
    out_ref[...] = res[:, 0:c3].astype(BF16)


def decode(x1, dev_index, num_dev, conv_in_weight, conv_in_bias, gain_in, up_weight, up_bias, gain_up, out_weight, out_bias):
    frames, rows1, cols, _ = x1.shape
    lat_rows = rows1 - 2
    lat_ch, c1 = conv_in_weight.shape[3:]
    c2, c3 = out_weight.shape[3:]
    taps = conv_in_weight[1:]
    none = jnp.zeros_like(taps[:, :, :1])
    w1 = jnp.stack(
        [jnp.concatenate([taps, none], axis=2), jnp.concatenate([none, taps], axis=2)], axis=4
    ).reshape(2, 12 * lat_ch, 2 * c1)
    wide = up_weight.astype(F32)
    by_row = jnp.stack(
        [jnp.stack([wide[0], wide[1] + wide[2]]), jnp.stack([wide[0] + wide[1], wide[2]])]
    )
    by_col = jnp.stack(
        [
            jnp.stack([by_row[:, :, 0], by_row[:, :, 1] + by_row[:, :, 2]], axis=2),
            jnp.stack([by_row[:, :, 0] + by_row[:, :, 1], by_row[:, :, 2]], axis=2),
        ],
        axis=2,
    )
    w2 = by_col.astype(BF16).reshape(2, 2, 2, 2 * c1, c2)
    w3 = jnp.pad(out_weight[1:], ((0, 0), (0, 0), (0, 0), (0, 256 - c2), (0, 128 - c3)))
    w3 = jnp.concatenate([w3[1], w3[0]], axis=-1).reshape(3, 768, 256)
    b3 = jnp.pad(out_bias, (0, 128 - c3))[None]
    cells = frames * 2 * lat_rows * 4 * cols
    vmem = pl.BlockSpec(memory_space=pltpu.VMEM)
    out = pl.pallas_call(
        functools.partial(conv_kernel, num_dev, lat_rows, (c1, c2, c3)),
        out_shape=jax.ShapeDtypeStruct((cells, c3), BF16),
        in_specs=[pl.BlockSpec(memory_space=pltpu.SMEM)] + [vmem] * 9,
        out_specs=vmem,
        scratch_shapes=[
            pltpu.VMEM((frames, rows1, cols, 4 * c1), BF16),
            pltpu.VMEM((frames, 2 * lat_rows + 2, cols, 6 * 256), BF16),
            pltpu.VMEM((cells, 128), F32),
        ],
        compiler_params=pltpu.CompilerParams(vmem_limit_bytes=40 * 1024 * 1024),
    )(dev_index[None].astype(jnp.int32), x1, w1, conv_in_bias[None], gain_in[None], w2, up_bias[None], gain_up[None], w3, b3)
    return out.reshape(frames, 2 * lat_rows, 4 * cols, c3)


def split3(weight):
    high = lax.reduce_precision(weight, 8, 7)
    rest = weight - high
    mid = lax.reduce_precision(rest, 8, 7)
    return jnp.concatenate([high.astype(BF16), mid.astype(BF16), (rest - mid).astype(BF16)], axis=0)


def local(
    hidden, mod_shift, mod_scale, head_weight, head_bias, conv_in_weight, conv_in_bias, gain_in,
    up_weight, up_bias, gain_up, out_weight, out_bias,
):
    num_dev = lax.axis_size("seq")
    dev_index = lax.axis_index("seq")
    frames, feat, tok_total = hidden.shape
    tile = tok_total // num_dev
    rows_dev = tile // TOK_W
    patch = head_weight.shape[0]
    lat_ch = patch // 4
    scaled = head_weight * (1.0 + mod_scale)
    sums = jnp.sum(scaled.reshape(patch, num_dev, feat), axis=2)
    base = jnp.sum(head_weight * mod_shift, axis=1) + head_bias

    mine = lax.dynamic_slice_in_dim(scaled, dev_index * feat, feat, axis=1)
    parts = jnp.einsum("fdt,kd->ftk", hidden, split3(mine), preferred_element_type=F32)
    values = hidden.astype(F32)
    mean = jnp.mean(values, axis=1)
    centred = values - mean[:, None]
    spread = jnp.sum(centred * centred, axis=1)
    part = parts[..., :patch] + (parts[..., patch : 2 * patch] + parts[..., 2 * patch :])
    part = part - mean[..., None] * lax.dynamic_slice_in_dim(sums, dev_index, 1, axis=1)[:, 0]
    part = part.reshape(frames, num_dev, tile, patch).transpose(1, 2, 0, 3).reshape(num_dev, tile, frames * patch)
    stats = jnp.stack([mean, spread]).reshape(2 * frames, num_dev, tile).transpose(1, 0, 2)
    stats = jnp.pad(stats, ((0, 0), (0, 8 - 2 * frames), (0, frames * patch - tile)))
    sent = jnp.concatenate([part, stats], axis=1)
    got = lax.all_to_all(sent, "seq", split_axis=0, concat_axis=0, tiled=True)

    got_part = got[:, :tile].reshape(num_dev, tile, frames, patch)
    got_stat = got[:, tile : tile + 2 * frames, :tile].reshape(num_dev, 2, frames, tile)
    means = got_stat[:, 0]
    total_mean = jnp.mean(means, axis=0)
    off = means - total_mean
    var = (jnp.sum(got_stat[:, 1], axis=0) + feat * jnp.sum(off * off, axis=0)) / (feat * num_dev)
    fixed = jnp.sum(off[..., None] * sums.T[:, None, None, :], axis=0)
    summed = jnp.sum(got_part, axis=0).transpose(1, 0, 2) + fixed
    projected = (summed * lax.rsqrt(var + 1e-06)[..., None] + base).astype(BF16)
    projected = projected.reshape(frames, rows_dev, TOK_W, patch)

    forward = [(i, i + 1) for i in range(num_dev - 1)]
    backward = [(j, i) for i, j in forward]
    low = lax.ppermute(projected[:, -1:], "seq", forward)
    high = lax.ppermute(projected[:, :1], "seq", backward)
    rows = jnp.concatenate([low, projected, high], axis=1)
    latent = rows.reshape(frames, rows_dev + 2, TOK_W, 2, 2 * lat_ch).transpose(0, 1, 3, 2, 4)
    latent = latent.reshape(frames, 2 * rows_dev + 4, TOK_W, 2 * lat_ch)
    left = jnp.pad(latent[:, :, :-1, lat_ch:], ((0, 0), (0, 0), (1, 0), (0, 0)))
    right = jnp.pad(latent[:, :, 1:, :lat_ch], ((0, 0), (0, 0), (0, 1), (0, 0)))
    quad = jnp.concatenate([left, latent, right], axis=-1)
    out_rows = 2 * rows_dev + 2
    x1 = jnp.concatenate([quad[:, b : b + out_rows] for b in range(3)], axis=-1)
    return decode(x1, dev_index, num_dev, conv_in_weight, conv_in_bias, gain_in, up_weight, up_bias, gain_up, out_weight, out_bias)


def solution(mesh):
    placed = (P("grp", "seq", None), P(), P(), P(), P(), P(), P(), P(), P(), P(), P(), P(), P())
    return jax.shard_map(
        local, mesh=mesh, in_specs=placed, out_specs=P("grp", "seq", None, None), check_vma=False
    )
```

```python
import functools

import jax
import jax.numpy as jnp
from jax import lax
from jax.experimental import pallas as pl
from jax.experimental.pallas import tpu as pltpu
from jax.sharding import PartitionSpec as P

TOK_W = 80
HIGH = lax.Precision.HIGHEST
F32 = jnp.float32
BF16 = jnp.bfloat16


def rms_silu(values, gain_vec):
    squares = jnp.mean(values * values, axis=-1, keepdims=True)
    normed = values * lax.rsqrt(squares + 1e-06) * gain_vec
    return normed * jax.nn.sigmoid(normed)


def shift_cols(values, step):
    count = values.shape[0]
    col = lax.broadcasted_iota(jnp.int32, (count, 1), 0) % TOK_W
    if step > 0:
        return jnp.where(col == 0, 0.0, pltpu.roll(values, 1, 0))
    return jnp.where(col == TOK_W - 1, 0.0, pltpu.roll(values, count - 1, 0))


def conv_kernel(num_dev, lat_rows, chans, pos_ref, x_ref, w1_ref, b1_ref, g1_ref, w2_ref, b2_ref, g2_ref,
                w3_ref, b3_ref, out_ref, act1, act2, res, w1s):
    c1, c2, c3 = chans
    ch = w1_ref.shape[3]
    blank = jnp.zeros((ch, c1), BF16)
    for a in range(2):
        for b in range(3):
            for j in range(4):
                rows = slice((4 * b + j) * ch, (4 * b + j + 1) * ch)
                w1s[a, rows, 0:c1] = w1_ref[a + 1, b, j] if j < 3 else blank
                w1s[a, rows, c1 : 2 * c1] = w1_ref[a + 1, b, j - 1] if j > 0 else blank
    dev = pos_ref[0]
    rows1 = lat_rows + 2
    m1 = rows1 * TOK_W
    rows2 = lat_rows + 1
    m2 = rows2 * TOK_W
    rows3 = 2 * lat_rows
    m3 = rows3 * TOK_W

    def inside(count, first, step, total):
        row = lax.broadcasted_iota(jnp.int32, (count, 1), 0) // TOK_W * step + first
        return (row >= 0) & (row < total)

    keep1 = inside(m1, dev * lat_rows - 1, 1, num_dev * lat_rows)
    for frame in range(2):
        x_now = x_ref[frame].reshape(m1, x_ref.shape[-1])
        pre = jnp.dot(x_now, w1s[1], preferred_element_type=F32)
        if frame == 1:
            x_old = x_ref[0].reshape(m1, x_ref.shape[-1])
            pre = pre + jnp.dot(x_old, w1s[0], preferred_element_type=F32)
        for r in range(2):
            val = rms_silu(pre[:, r * c1 : (r + 1) * c1] + b1_ref[...], g1_ref[...])
            val = jnp.where(keep1, val, 0.0)
            edge = shift_cols(val, 1) if r == 1 else shift_cols(val, -1)
            spot = 0 if r == 1 else 3
            act1[frame, :, :, (r + 1) * c1 : (r + 2) * c1] = val.astype(BF16).reshape(rows1, TOK_W, c1)
            act1[frame, :, :, spot * c1 : (spot + 1) * c1] = edge.astype(BF16).reshape(rows1, TOK_W, c1)

    start = (0, 1, 1, 2)
    for p in range(2):
        first = 0 if p == 0 else -1
        keep2 = inside(m2, 2 * dev * lat_rows + first, 2, 2 * num_dev * lat_rows)
        for frame in range(2):
            for s in range(4):
                q = s % 2
                lanes = slice(start[s] * c1, (start[s] + 2) * c1)
                top = act1[frame, 0:rows2, :, lanes].reshape(m2, 2 * c1)
                low = act1[frame, 1 : rows2 + 1, :, lanes].reshape(m2, 2 * c1)
                pre = jnp.dot(top, w2_ref[p, 0, q], preferred_element_type=F32)
                pre = pre + jnp.dot(low, w2_ref[p, 1, q], preferred_element_type=F32)
                val = rms_silu(pre + b2_ref[...], g2_ref[...])
                val = jnp.where(keep2, val, 0.0)
                val = jnp.concatenate([val, jnp.zeros((m2, 256 - c2), F32)], axis=1)
                pieces = [(s + 1, val)]
                if s == 3:
                    pieces.append((0, shift_cols(val, 1)))
                if s == 0:
                    pieces.append((5, shift_cols(val, -1)))
                for spot, piece in pieces:
                    piece = piece.astype(BF16).reshape(rows2, TOK_W, 256)
                    for i in range(rows2):
                        act2[frame, 2 * i + 1 - p, :, spot * 256 : (spot + 1) * 256] = piece[i]

    for s in range(4):
        lanes = slice(s * 256, (s + 3) * 256)
        old = None
        new = None
        for b in range(3):
            before = act2[0, b : b + rows3, :, lanes].reshape(m3, 768)
            after = act2[1, b : b + rows3, :, lanes].reshape(m3, 768)
            one = jnp.dot(before, w3_ref[b], preferred_element_type=F32)
            two = jnp.dot(after, w3_ref[b, :, 0:128], preferred_element_type=F32)
            old = one if old is None else old + one
            new = two if new is None else new + two
        res[pl.ds(s, m3, stride=4), :] = old[:, 0:128] + b3_ref[...]
        res[pl.ds(4 * m3 + s, m3, stride=4), :] = old[:, 128:256] + new + b3_ref[...]
    width = 4 * TOK_W
    for i in range(2 * rows3):
        out_ref[i] = jnp.transpose(res[i * width : (i + 1) * width, :])[0:c3].astype(BF16)


def decode(x1, dev_index, num_dev, conv_in_weight, conv_in_bias, gain_in, up_weight, up_bias, gain_up, out_weight, out_bias):
    frames, rows1, cols, _ = x1.shape
    lat_rows = rows1 - 2
    lat_ch, c1 = conv_in_weight.shape[3:]
    c2, c3 = out_weight.shape[3:]
    wide = up_weight.astype(F32)
    by_row = jnp.stack(
        [jnp.stack([wide[0], wide[1] + wide[2]]), jnp.stack([wide[0] + wide[1], wide[2]])]
    )
    by_col = jnp.stack(
        [
            jnp.stack([by_row[:, :, 0], by_row[:, :, 1] + by_row[:, :, 2]], axis=2),
            jnp.stack([by_row[:, :, 0] + by_row[:, :, 1], by_row[:, :, 2]], axis=2),
        ],
        axis=2,
    )
    w2 = by_col.astype(BF16).reshape(2, 2, 2, 2 * c1, c2)
    w3 = jnp.pad(out_weight[1:], ((0, 0), (0, 0), (0, 0), (0, 256 - c2), (0, 128 - c3)))
    w3 = jnp.concatenate([w3[1], w3[0]], axis=-1).reshape(3, 768, 256)
    b3 = jnp.pad(out_bias, (0, 128 - c3))[None]
    cells = frames * 2 * lat_rows * 4 * cols
    vmem = pl.BlockSpec(memory_space=pltpu.VMEM)
    out = pl.pallas_call(
        functools.partial(conv_kernel, num_dev, lat_rows, (c1, c2, c3)),
        out_shape=jax.ShapeDtypeStruct((frames * 2 * lat_rows, c3, 4 * cols), BF16),
        in_specs=[pl.BlockSpec(memory_space=pltpu.SMEM)] + [vmem] * 9,
        out_specs=vmem,
        scratch_shapes=[
            pltpu.VMEM((frames, rows1, cols, 4 * c1), BF16),
            pltpu.VMEM((frames, 2 * lat_rows + 2, cols, 6 * 256), BF16),
            pltpu.VMEM((cells, 128), F32),
            pltpu.VMEM((2, 12 * lat_ch, 2 * c1), BF16),
        ],
        compiler_params=pltpu.CompilerParams(vmem_limit_bytes=40 * 1024 * 1024),
    )(dev_index[None].astype(jnp.int32), x1, conv_in_weight, conv_in_bias[None], gain_in[None], w2, up_bias[None], gain_up[None], w3, b3)
    return out.reshape(frames, 2 * lat_rows, c3, 4 * cols).transpose(0, 1, 3, 2)


def split3(weight):
    high = lax.reduce_precision(weight, 8, 7)
    rest = weight - high
    mid = lax.reduce_precision(rest, 8, 7)
    return jnp.concatenate([high.astype(BF16), mid.astype(BF16), (rest - mid).astype(BF16)], axis=0)


def local(
    hidden, mod_shift, mod_scale, head_weight, head_bias, conv_in_weight, conv_in_bias, gain_in,
    up_weight, up_bias, gain_up, out_weight, out_bias,
):
    num_dev = lax.axis_size("seq")
    dev_index = lax.axis_index("seq")
    frames, feat, tok_total = hidden.shape
    tile = tok_total // num_dev
    rows_dev = tile // TOK_W
    patch = head_weight.shape[0]
    lat_ch = patch // 4
    scaled = head_weight * (1.0 + mod_scale)
    sums = jnp.sum(scaled.reshape(patch, num_dev, feat), axis=2)
    base = jnp.sum(head_weight * mod_shift, axis=1) + head_bias

    mine = lax.dynamic_slice_in_dim(scaled, dev_index * feat, feat, axis=1)
    parts = jnp.einsum("fdt,kd->ftk", hidden, split3(mine), preferred_element_type=F32)
    values = hidden.astype(F32)
    mean = jnp.mean(values, axis=1)
    centred = values - mean[:, None]
    spread = jnp.sum(centred * centred, axis=1)
    part = parts[..., :patch] + (parts[..., patch : 2 * patch] + parts[..., 2 * patch :])
    part = part - mean[..., None] * jnp.sum(mine, axis=1)
    part = part.reshape(frames, num_dev, tile, patch).transpose(1, 2, 0, 3).reshape(num_dev, tile, frames * patch)
    stats = jnp.stack([mean, spread]).reshape(2 * frames, num_dev, tile).transpose(1, 0, 2)
    stats = jnp.pad(stats, ((0, 0), (0, 8 - 2 * frames), (0, frames * patch - tile)))
    sent = jnp.concatenate([part, stats], axis=1)
    got = lax.all_to_all(sent, "seq", split_axis=0, concat_axis=0, tiled=True)

    got_part = got[:, :tile].reshape(num_dev, tile, frames, patch)
    got_stat = got[:, tile : tile + 2 * frames, :tile].reshape(num_dev, 2, frames, tile)
    means = got_stat[:, 0]
    total_mean = jnp.mean(means, axis=0)
    off = means - total_mean
    var = (jnp.sum(got_stat[:, 1], axis=0) + feat * jnp.sum(off * off, axis=0)) / (feat * num_dev)
    fixed = jnp.sum(off[..., None] * sums.T[:, None, None, :], axis=0)
    summed = jnp.sum(got_part, axis=0).transpose(1, 0, 2) + fixed
    projected = (summed * lax.rsqrt(var + 1e-06)[..., None] + base).astype(BF16)
    projected = projected.reshape(frames, rows_dev, TOK_W, patch)

    forward = [(i, i + 1) for i in range(num_dev - 1)]
    backward = [(j, i) for i, j in forward]
    low = lax.ppermute(projected[:, -1:], "seq", forward)
    high = lax.ppermute(projected[:, :1], "seq", backward)
    rows = jnp.concatenate([low, projected, high], axis=1)
    latent = rows.reshape(frames, rows_dev + 2, TOK_W, 2, 2 * lat_ch).transpose(0, 1, 3, 2, 4)
    latent = latent.reshape(frames, 2 * rows_dev + 4, TOK_W, 2 * lat_ch)
    left = jnp.pad(latent[:, :, :-1, lat_ch:], ((0, 0), (0, 0), (1, 0), (0, 0)))
    right = jnp.pad(latent[:, :, 1:, :lat_ch], ((0, 0), (0, 0), (0, 1), (0, 0)))
    quad = jnp.concatenate([left, latent, right], axis=-1)
    out_rows = 2 * rows_dev + 2
    x1 = jnp.concatenate([quad[:, b : b + out_rows] for b in range(3)], axis=-1)
    return decode(x1, dev_index, num_dev, conv_in_weight, conv_in_bias, gain_in, up_weight, up_bias, gain_up, out_weight, out_bias)


def solution(mesh):
    placed = (P("grp", "seq", None), P(), P(), P(), P(), P(), P(), P(), P(), P(), P(), P(), P())
    return jax.shard_map(
        local, mesh=mesh, in_specs=placed, out_specs=P("grp", "seq", None, None), check_vma=False
    )
```

```python
import functools

import jax
import jax.numpy as jnp
from jax import lax
from jax.experimental import pallas as pl
from jax.experimental.pallas import tpu as pltpu
from jax.sharding import PartitionSpec as P

TOK_W = 80
HIGH = lax.Precision.HIGHEST
F32 = jnp.float32
BF16 = jnp.bfloat16


def rms_silu(values, gain_vec):
    squares = jnp.mean(values * values, axis=-1, keepdims=True)
    normed = values * lax.rsqrt(squares + 1e-06) * gain_vec
    return normed * jax.nn.sigmoid(normed)


def shift_cols(values, step):
    count = values.shape[0]
    col = lax.broadcasted_iota(jnp.int32, (count, 1), 0) % TOK_W
    if step > 0:
        return jnp.where(col == 0, 0.0, pltpu.roll(values, 1, 0))
    return jnp.where(col == TOK_W - 1, 0.0, pltpu.roll(values, count - 1, 0))


def conv_kernel(num_dev, lat_rows, chans, pos_ref, x_ref, w1_ref, b1_ref, g1_ref, w2_ref, b2_ref, g2_ref,
                w3_ref, b3_ref, out_ref, act1, act2, res, w1s):
    c1, c2, c3 = chans
    ch = w1_ref.shape[3]
    blank = jnp.zeros((ch, c1), BF16)
    for a in range(2):
        for b in range(3):
            for j in range(4):
                rows = slice((4 * b + j) * ch, (4 * b + j + 1) * ch)
                w1s[a, rows, 0:c1] = w1_ref[a + 1, b, j] if j < 3 else blank
                w1s[a, rows, c1 : 2 * c1] = w1_ref[a + 1, b, j - 1] if j > 0 else blank
    dev = pos_ref[0]
    rows1 = lat_rows + 2
    m1 = rows1 * TOK_W
    rows2 = lat_rows + 1
    m2 = rows2 * TOK_W
    rows3 = 2 * lat_rows
    m3 = rows3 * TOK_W

    def inside(count, first, step, total):
        row = lax.broadcasted_iota(jnp.int32, (count, 1), 0) // TOK_W * step + first
        return (row >= 0) & (row < total)

    keep1 = inside(m1, dev * lat_rows - 1, 1, num_dev * lat_rows)
    for frame in range(2):
        x_now = x_ref[frame].reshape(m1, x_ref.shape[-1])
        pre = jnp.dot(x_now, w1s[1], preferred_element_type=F32)
        if frame == 1:
            x_old = x_ref[0].reshape(m1, x_ref.shape[-1])
            pre = pre + jnp.dot(x_old, w1s[0], preferred_element_type=F32)
        for r in range(2):
            val = rms_silu(pre[:, r * c1 : (r + 1) * c1] + b1_ref[...], g1_ref[...])
            val = jnp.where(keep1, val, 0.0)
            edge = shift_cols(val, 1) if r == 1 else shift_cols(val, -1)
            spot = 0 if r == 1 else 3
            act1[frame, :, :, (r + 1) * c1 : (r + 2) * c1] = val.astype(BF16).reshape(rows1, TOK_W, c1)
            act1[frame, :, :, spot * c1 : (spot + 1) * c1] = edge.astype(BF16).reshape(rows1, TOK_W, c1)

    start = (0, 1, 1, 2)
    for p in range(2):
        first = 0 if p == 0 else -1
        keep2 = inside(m2, 2 * dev * lat_rows + first, 2, 2 * num_dev * lat_rows)
        for frame in range(2):
            for s in range(4):
                q = s % 2
                lanes = slice(start[s] * c1, (start[s] + 2) * c1)
                top = act1[frame, 0:rows2, :, lanes].reshape(m2, 2 * c1)
                low = act1[frame, 1 : rows2 + 1, :, lanes].reshape(m2, 2 * c1)
                pre = jnp.dot(top, w2_ref[p, 0, q], preferred_element_type=F32)
                pre = pre + jnp.dot(low, w2_ref[p, 1, q], preferred_element_type=F32)
                val = rms_silu(pre + b2_ref[...], g2_ref[...])
                val = jnp.where(keep2, val, 0.0)
                val = jnp.concatenate([val, jnp.zeros((m2, 256 - c2), F32)], axis=1)
                pieces = [(s + 1, val)]
                if s == 3:
                    pieces.append((0, shift_cols(val, 1)))
                if s == 0:
                    pieces.append((5, shift_cols(val, -1)))
                for spot, piece in pieces:
                    piece = piece.astype(BF16).reshape(rows2, TOK_W, 256)
                    for i in range(rows2):
                        act2[frame, 2 * i + 1 - p, :, spot * 256 : (spot + 1) * 256] = piece[i]

    for s in range(4):
        lanes = slice(s * 256, (s + 3) * 256)
        old = None
        new = None
        for b in range(3):
            before = act2[0, b : b + rows3, :, lanes].reshape(m3, 768)
            after = act2[1, b : b + rows3, :, lanes].reshape(m3, 768)
            one = jnp.dot(before, w3_ref[b], preferred_element_type=F32)
            two = jnp.dot(after, w3_ref[b, :, 0:128], preferred_element_type=F32)
            old = one if old is None else old + one
            new = two if new is None else new + two
        res[pl.ds(s, m3, stride=4), :] = old[:, 0:128] + b3_ref[...]
        res[pl.ds(4 * m3 + s, m3, stride=4), :] = old[:, 128:256] + new + b3_ref[...]
    width = 4 * TOK_W
    for i in range(2 * rows3):
        out_ref[i] = jnp.transpose(res[i * width : (i + 1) * width, :])[0:c3].astype(BF16)


def decode(x1, dev_index, num_dev, conv_in_weight, conv_in_bias, gain_in, up_weight, up_bias, gain_up, out_weight, out_bias):
    frames, rows1, cols, _ = x1.shape
    lat_rows = rows1 - 2
    lat_ch, c1 = conv_in_weight.shape[3:]
    c2, c3 = out_weight.shape[3:]
    wide = up_weight.astype(F32)
    by_row = jnp.stack(
        [jnp.stack([wide[0], wide[1] + wide[2]]), jnp.stack([wide[0] + wide[1], wide[2]])]
    )
    by_col = jnp.stack(
        [
            jnp.stack([by_row[:, :, 0], by_row[:, :, 1] + by_row[:, :, 2]], axis=2),
            jnp.stack([by_row[:, :, 0] + by_row[:, :, 1], by_row[:, :, 2]], axis=2),
        ],
        axis=2,
    )
    w2 = by_col.astype(BF16).reshape(2, 2, 2, 2 * c1, c2)
    w3 = jnp.pad(out_weight[1:], ((0, 0), (0, 0), (0, 0), (0, 256 - c2), (0, 128 - c3)))
    w3 = jnp.concatenate([w3[1], w3[0]], axis=-1).reshape(3, 768, 256)
    b3 = jnp.pad(out_bias, (0, 128 - c3))[None]
    cells = frames * 2 * lat_rows * 4 * cols
    vmem = pl.BlockSpec(memory_space=pltpu.VMEM)
    out = pl.pallas_call(
        functools.partial(conv_kernel, num_dev, lat_rows, (c1, c2, c3)),
        out_shape=jax.ShapeDtypeStruct((frames * 2 * lat_rows, c3, 4 * cols), BF16),
        in_specs=[pl.BlockSpec(memory_space=pltpu.SMEM)] + [vmem] * 9,
        out_specs=vmem,
        scratch_shapes=[
            pltpu.VMEM((frames, rows1, cols, 4 * c1), BF16),
            pltpu.VMEM((frames, 2 * lat_rows + 2, cols, 6 * 256), BF16),
            pltpu.VMEM((cells, 128), F32),
            pltpu.VMEM((2, 12 * lat_ch, 2 * c1), BF16),
        ],
        compiler_params=pltpu.CompilerParams(vmem_limit_bytes=40 * 1024 * 1024),
    )(dev_index[None].astype(jnp.int32), x1, conv_in_weight, conv_in_bias[None], gain_in[None], w2, up_bias[None], gain_up[None], w3, b3)
    return out.reshape(frames, 2 * lat_rows, c3, 4 * cols).transpose(0, 1, 3, 2)


def head_kernel(num_dev, x_ref, w_ref, out_ref):
    frames, feat, total = x_ref.shape
    tile = total // num_dev
    weight = w_ref[...]
    patch = weight.shape[0]
    high = weight.astype(BF16)
    rest = weight - high.astype(F32)
    mid = rest.astype(BF16)
    low = (rest - mid.astype(F32)).astype(BF16)
    stack = jnp.concatenate([high, mid, low], axis=0)
    sums = jnp.sum(weight, axis=1, keepdims=True)
    parts, means, spreads = [], [], []
    for f in range(frames):
        full = jnp.dot(stack, x_ref[f], preferred_element_type=F32)
        values = x_ref[f].astype(F32)
        mean = jnp.sum(values, axis=0, keepdims=True) * (1.0 / feat)
        centred = values - mean
        means.append(mean)
        spreads.append(jnp.sum(centred * centred, axis=0, keepdims=True))
        part = full[:patch] + (full[patch : 2 * patch] + full[2 * patch :])
        parts.append(part - sums * mean)
    both = jnp.concatenate(parts, axis=0)
    out_ref[:, 0:tile, :] = jnp.transpose(both).reshape(num_dev, tile, frames * patch)
    out_ref[:, tile : tile + 8, :] = jnp.zeros((num_dev, 8, frames * patch), F32)
    stats = jnp.concatenate(means + spreads, axis=0)
    for i in range(num_dev):
        out_ref[i, tile : tile + 2 * frames, 0:tile] = stats[:, i * tile : (i + 1) * tile]


def local(
    hidden, mod_shift, mod_scale, head_weight, head_bias, conv_in_weight, conv_in_bias, gain_in,
    up_weight, up_bias, gain_up, out_weight, out_bias,
):
    num_dev = lax.axis_size("seq")
    dev_index = lax.axis_index("seq")
    frames, feat, tok_total = hidden.shape
    tile = tok_total // num_dev
    rows_dev = tile // TOK_W
    patch = head_weight.shape[0]
    lat_ch = patch // 4
    scaled = head_weight * (1.0 + mod_scale)
    sums = jnp.sum(scaled.reshape(patch, num_dev, feat), axis=2)
    base = jnp.sum(head_weight * mod_shift, axis=1) + head_bias

    mine = lax.dynamic_slice_in_dim(head_weight, dev_index * feat, feat, axis=1)
    mine = mine * (1.0 + lax.dynamic_slice_in_dim(mod_scale, dev_index * feat, feat))
    vmem = pl.BlockSpec(memory_space=pltpu.VMEM)
    sent = pl.pallas_call(
        functools.partial(head_kernel, num_dev),
        out_shape=jax.ShapeDtypeStruct((num_dev, tile + 8, frames * patch), F32),
        in_specs=[vmem, vmem],
        out_specs=vmem,
        compiler_params=pltpu.CompilerParams(vmem_limit_bytes=40 * 1024 * 1024),
    )(hidden, mine)
    got = lax.all_to_all(sent, "seq", split_axis=0, concat_axis=0, tiled=True)

    got_part = got[:, :tile].reshape(num_dev, tile, frames, patch)
    got_stat = got[:, tile : tile + 2 * frames, :tile].reshape(num_dev, 2, frames, tile)
    means = got_stat[:, 0]
    total_mean = jnp.mean(means, axis=0)
    off = means - total_mean
    var = (jnp.sum(got_stat[:, 1], axis=0) + feat * jnp.sum(off * off, axis=0)) / (feat * num_dev)
    fixed = jnp.sum(off[..., None] * sums.T[:, None, None, :], axis=0)
    summed = jnp.sum(got_part, axis=0).transpose(1, 0, 2) + fixed
    projected = (summed * lax.rsqrt(var + 1e-06)[..., None] + base).astype(BF16)
    projected = projected.reshape(frames, rows_dev, TOK_W, patch)

    forward = [(i, i + 1) for i in range(num_dev - 1)]
    backward = [(j, i) for i, j in forward]
    low = lax.ppermute(projected[:, -1:], "seq", forward)
    high = lax.ppermute(projected[:, :1], "seq", backward)
    rows = jnp.concatenate([low, projected, high], axis=1)
    latent = rows.reshape(frames, rows_dev + 2, TOK_W, 2, 2 * lat_ch).transpose(0, 1, 3, 2, 4)
    latent = latent.reshape(frames, 2 * rows_dev + 4, TOK_W, 2 * lat_ch)
    left = jnp.pad(latent[:, :, :-1, lat_ch:], ((0, 0), (0, 0), (1, 0), (0, 0)))
    right = jnp.pad(latent[:, :, 1:, :lat_ch], ((0, 0), (0, 0), (0, 1), (0, 0)))
    quad = jnp.concatenate([left, latent, right], axis=-1)
    out_rows = 2 * rows_dev + 2
    x1 = jnp.concatenate([quad[:, b : b + out_rows] for b in range(3)], axis=-1)
    return decode(x1, dev_index, num_dev, conv_in_weight, conv_in_bias, gain_in, up_weight, up_bias, gain_up, out_weight, out_bias)


def solution(mesh):
    placed = (P("grp", "seq", None), P(), P(), P(), P(), P(), P(), P(), P(), P(), P(), P(), P())
    return jax.shard_map(
        local, mesh=mesh, in_specs=placed, out_specs=P("grp", "seq", None, None), check_vma=False
    )
```

```python
import functools

import jax
import jax.numpy as jnp
from jax import lax
from jax.experimental import pallas as pl
from jax.experimental.pallas import tpu as pltpu
from jax.sharding import PartitionSpec as P

TOK_W = 80
HIGH = lax.Precision.HIGHEST
F32 = jnp.float32
BF16 = jnp.bfloat16


def rms_silu(values, gain_vec):
    squares = jnp.mean(values * values, axis=-1, keepdims=True)
    normed = values * lax.rsqrt(squares + 1e-06) * gain_vec
    return normed * jax.nn.sigmoid(normed)


def shift_cols(values, step):
    count = values.shape[0]
    col = lax.broadcasted_iota(jnp.int32, (count, 1), 0) % TOK_W
    if step > 0:
        return jnp.where(col == 0, 0.0, pltpu.roll(values, 1, 0))
    return jnp.where(col == TOK_W - 1, 0.0, pltpu.roll(values, count - 1, 0))


def conv_kernel(num_dev, lat_rows, chans, pos_ref, x_ref, w1_ref, b1_ref, g1_ref, w2_ref, b2_ref, g2_ref,
                w3_ref, b3_ref, out_ref, act1, act2, res, w1s):
    c1, c2, c3 = chans
    ch = w1_ref.shape[3]
    blank = jnp.zeros((ch, c1), BF16)
    for a in range(2):
        for b in range(3):
            for j in range(4):
                rows = slice((4 * b + j) * ch, (4 * b + j + 1) * ch)
                w1s[a, rows, 0:c1] = w1_ref[a + 1, b, j] if j < 3 else blank
                w1s[a, rows, c1 : 2 * c1] = w1_ref[a + 1, b, j - 1] if j > 0 else blank
    dev = pos_ref[0]
    rows1 = lat_rows + 2
    m1 = rows1 * TOK_W
    rows2 = lat_rows + 1
    m2 = rows2 * TOK_W
    rows3 = 2 * lat_rows
    m3 = rows3 * TOK_W

    def inside(count, first, step, total):
        row = lax.broadcasted_iota(jnp.int32, (count, 1), 0) // TOK_W * step + first
        return (row >= 0) & (row < total)

    keep1 = inside(m1, dev * lat_rows - 1, 1, num_dev * lat_rows)
    for frame in range(2):
        x_now = x_ref[frame].reshape(m1, x_ref.shape[-1])
        pre = jnp.dot(x_now, w1s[1], preferred_element_type=F32)
        if frame == 1:
            x_old = x_ref[0].reshape(m1, x_ref.shape[-1])
            pre = pre + jnp.dot(x_old, w1s[0], preferred_element_type=F32)
        for r in range(2):
            val = rms_silu(pre[:, r * c1 : (r + 1) * c1] + b1_ref[...], g1_ref[...])
            val = jnp.where(keep1, val, 0.0)
            edge = shift_cols(val, 1) if r == 1 else shift_cols(val, -1)
            spot = 0 if r == 1 else 3
            act1[frame, :, :, (r + 1) * c1 : (r + 2) * c1] = val.astype(BF16).reshape(rows1, TOK_W, c1)
            act1[frame, :, :, spot * c1 : (spot + 1) * c1] = edge.astype(BF16).reshape(rows1, TOK_W, c1)

    start = (0, 1, 1, 2)
    for p in range(2):
        first = 0 if p == 0 else -1
        keep2 = inside(m2, 2 * dev * lat_rows + first, 2, 2 * num_dev * lat_rows)
        for frame in range(2):
            for s in range(4):
                q = s % 2
                lanes = slice(start[s] * c1, (start[s] + 2) * c1)
                top = act1[frame, 0:rows2, :, lanes].reshape(m2, 2 * c1)
                low = act1[frame, 1 : rows2 + 1, :, lanes].reshape(m2, 2 * c1)
                pre = jnp.dot(top, w2_ref[p, 0, q], preferred_element_type=F32)
                pre = pre + jnp.dot(low, w2_ref[p, 1, q], preferred_element_type=F32)
                val = rms_silu(pre + b2_ref[...], g2_ref[...])
                val = jnp.where(keep2, val, 0.0)
                val = jnp.concatenate([val, jnp.zeros((m2, 256 - c2), F32)], axis=1)
                pieces = [(s + 1, val)]
                if s == 3:
                    pieces.append((0, shift_cols(val, 1)))
                if s == 0:
                    pieces.append((5, shift_cols(val, -1)))
                for spot, piece in pieces:
                    piece = piece.astype(BF16).reshape(rows2, TOK_W, 256)
                    for i in range(rows2):
                        act2[frame, 2 * i + 1 - p, :, spot * 256 : (spot + 1) * 256] = piece[i]

    for s in range(4):
        lanes = slice(s * 256, (s + 3) * 256)
        old = None
        new = None
        for b in range(3):
            before = act2[0, b : b + rows3, :, lanes].reshape(m3, 768)
            after = act2[1, b : b + rows3, :, lanes].reshape(m3, 768)
            one = jnp.dot(before, w3_ref[b], preferred_element_type=F32)
            two = jnp.dot(after, w3_ref[b, :, 0:128], preferred_element_type=F32)
            old = one if old is None else old + one
            new = two if new is None else new + two
        res[pl.ds(s, m3, stride=4), :] = old[:, 0:128] + b3_ref[...]
        res[pl.ds(4 * m3 + s, m3, stride=4), :] = old[:, 128:256] + new + b3_ref[...]
    width = 4 * TOK_W
    for i in range(2 * rows3):
        out_ref[i] = jnp.transpose(res[i * width : (i + 1) * width, :])[0:c3].astype(BF16)


def decode(x1, dev_index, num_dev, conv_in_weight, conv_in_bias, gain_in, up_weight, up_bias, gain_up, out_weight, out_bias):
    frames, rows1, cols, _ = x1.shape
    lat_rows = rows1 - 2
    lat_ch, c1 = conv_in_weight.shape[3:]
    c2, c3 = out_weight.shape[3:]
    wide = up_weight.astype(F32)
    by_row = jnp.stack(
        [jnp.stack([wide[0], wide[1] + wide[2]]), jnp.stack([wide[0] + wide[1], wide[2]])]
    )
    by_col = jnp.stack(
        [
            jnp.stack([by_row[:, :, 0], by_row[:, :, 1] + by_row[:, :, 2]], axis=2),
            jnp.stack([by_row[:, :, 0] + by_row[:, :, 1], by_row[:, :, 2]], axis=2),
        ],
        axis=2,
    )
    w2 = by_col.astype(BF16).reshape(2, 2, 2, 2 * c1, c2)
    w3 = jnp.pad(out_weight[1:], ((0, 0), (0, 0), (0, 0), (0, 256 - c2), (0, 128 - c3)))
    w3 = jnp.concatenate([w3[1], w3[0]], axis=-1).reshape(3, 768, 256)
    b3 = jnp.pad(out_bias, (0, 128 - c3))[None]
    cells = frames * 2 * lat_rows * 4 * cols
    vmem = pl.BlockSpec(memory_space=pltpu.VMEM)
    out = pl.pallas_call(
        functools.partial(conv_kernel, num_dev, lat_rows, (c1, c2, c3)),
        out_shape=jax.ShapeDtypeStruct((frames * 2 * lat_rows, c3, 4 * cols), BF16),
        in_specs=[pl.BlockSpec(memory_space=pltpu.SMEM)] + [vmem] * 9,
        out_specs=vmem,
        scratch_shapes=[
            pltpu.VMEM((frames, rows1, cols, 4 * c1), BF16),
            pltpu.VMEM((frames, 2 * lat_rows + 2, cols, 6 * 256), BF16),
            pltpu.VMEM((cells, 128), F32),
            pltpu.VMEM((2, 12 * lat_ch, 2 * c1), BF16),
        ],
        compiler_params=pltpu.CompilerParams(vmem_limit_bytes=40 * 1024 * 1024),
    )(dev_index[None].astype(jnp.int32), x1, conv_in_weight, conv_in_bias[None], gain_in[None], w2, up_bias[None], gain_up[None], w3, b3)
    return out.reshape(frames, 2 * lat_rows, c3, 4 * cols).transpose(0, 1, 3, 2)


def head_kernel(num_dev, x_ref, w_ref, out_ref):
    frames, feat, total = x_ref.shape
    tile = total // num_dev
    weight = w_ref[...]
    patch = weight.shape[0]
    high = weight.astype(BF16)
    rest = weight - high.astype(F32)
    mid = rest.astype(BF16)
    low = (rest - mid.astype(F32)).astype(BF16)
    stack = jnp.concatenate([high, mid, low], axis=0)
    sums = jnp.sum(weight, axis=1, keepdims=True)
    parts, means, spreads = [], [], []
    for f in range(frames):
        full = jnp.dot(stack, x_ref[f], preferred_element_type=F32)
        values = x_ref[f].astype(F32)
        mean = jnp.sum(values, axis=0, keepdims=True) * (1.0 / feat)
        centred = values - mean
        means.append(mean)
        spreads.append(jnp.sum(centred * centred, axis=0, keepdims=True))
        part = full[:patch] + (full[patch : 2 * patch] + full[2 * patch :])
        parts.append(part - sums * mean)
    both = jnp.concatenate(parts, axis=0)
    out_ref[:, 0:tile, :] = jnp.transpose(both).reshape(num_dev, tile, frames * patch)
    out_ref[:, tile : tile + 8, :] = jnp.zeros((num_dev, 8, frames * patch), F32)
    stats = jnp.concatenate(means + spreads, axis=0)
    for i in range(num_dev):
        out_ref[i, tile : tile + 2 * frames, 0:tile] = stats[:, i * tile : (i + 1) * tile]


def merge_kernel(feat, tile, got_ref, sums_ref, base_ref, out_ref):
    num_dev = got_ref.shape[0]
    patch = sums_ref.shape[1]
    for f in range(2):
        means = got_ref[:, tile + f, :]
        off = means - jnp.mean(means, axis=0, keepdims=True)
        spread = jnp.sum(got_ref[:, tile + 2 + f, :], axis=0, keepdims=True)
        var = (spread + feat * jnp.sum(off * off, axis=0, keepdims=True)) * (1.0 / (feat * num_dev))
        scale = jnp.transpose(jnp.broadcast_to(lax.rsqrt(var + 1e-06), (8, var.shape[1])))[0:tile, 0:1]
        fixed = jnp.dot(jnp.transpose(off), sums_ref[...], precision=HIGH, preferred_element_type=F32)
        summed = jnp.sum(got_ref[:, 0:tile, :], axis=0)[:, f * patch : (f + 1) * patch] + fixed[0:tile]
        out_ref[f] = (summed * scale + base_ref[...]).astype(BF16)


def local(
    hidden, mod_shift, mod_scale, head_weight, head_bias, conv_in_weight, conv_in_bias, gain_in,
    up_weight, up_bias, gain_up, out_weight, out_bias,
):
    num_dev = lax.axis_size("seq")
    dev_index = lax.axis_index("seq")
    frames, feat, tok_total = hidden.shape
    tile = tok_total // num_dev
    rows_dev = tile // TOK_W
    patch = head_weight.shape[0]
    lat_ch = patch // 4
    scaled = head_weight * (1.0 + mod_scale)
    sums = jnp.sum(scaled.reshape(patch, num_dev, feat), axis=2)
    base = jnp.sum(head_weight * mod_shift, axis=1) + head_bias

    mine = lax.dynamic_slice_in_dim(head_weight, dev_index * feat, feat, axis=1)
    mine = mine * (1.0 + lax.dynamic_slice_in_dim(mod_scale, dev_index * feat, feat))
    vmem = pl.BlockSpec(memory_space=pltpu.VMEM)
    sent = pl.pallas_call(
        functools.partial(head_kernel, num_dev),
        out_shape=jax.ShapeDtypeStruct((num_dev, tile + 8, frames * patch), F32),
        in_specs=[vmem, vmem],
        out_specs=vmem,
        compiler_params=pltpu.CompilerParams(vmem_limit_bytes=40 * 1024 * 1024),
    )(hidden, mine)
    got = lax.all_to_all(sent, "seq", split_axis=0, concat_axis=0, tiled=True)

    projected = pl.pallas_call(
        functools.partial(merge_kernel, feat, tile),
        out_shape=jax.ShapeDtypeStruct((frames, tile, patch), BF16),
        in_specs=[vmem] * 3,
        out_specs=vmem,
        compiler_params=pltpu.CompilerParams(vmem_limit_bytes=40 * 1024 * 1024),
    )(got, sums.T, base[None])
    projected = projected.reshape(frames, rows_dev, TOK_W, patch)

    forward = [(i, i + 1) for i in range(num_dev - 1)]
    backward = [(j, i) for i, j in forward]
    low = lax.ppermute(projected[:, -1:], "seq", forward)
    high = lax.ppermute(projected[:, :1], "seq", backward)
    rows = jnp.concatenate([low, projected, high], axis=1)
    latent = rows.reshape(frames, rows_dev + 2, TOK_W, 2, 2 * lat_ch).transpose(0, 1, 3, 2, 4)
    latent = latent.reshape(frames, 2 * rows_dev + 4, TOK_W, 2 * lat_ch)
    left = jnp.pad(latent[:, :, :-1, lat_ch:], ((0, 0), (0, 0), (1, 0), (0, 0)))
    right = jnp.pad(latent[:, :, 1:, :lat_ch], ((0, 0), (0, 0), (0, 1), (0, 0)))
    quad = jnp.concatenate([left, latent, right], axis=-1)
    out_rows = 2 * rows_dev + 2
    x1 = jnp.concatenate([quad[:, b : b + out_rows] for b in range(3)], axis=-1)
    return decode(x1, dev_index, num_dev, conv_in_weight, conv_in_bias, gain_in, up_weight, up_bias, gain_up, out_weight, out_bias)


def solution(mesh):
    placed = (P("grp", "seq", None), P(), P(), P(), P(), P(), P(), P(), P(), P(), P(), P(), P())
    return jax.shard_map(
        local, mesh=mesh, in_specs=placed, out_specs=P("grp", "seq", None, None), check_vma=False
    )
```
